32 devices in a mesh: dp: 8 (over z, x), comp: 4 (over y, core).
Axes of the slice: x: 2, y: 2, z: 4, core: 2. Of those that a mesh axis runs over, the one named last changes fastest.
Arguments:
- points: float32 [1024, 1024], P('dp'), may hold values from -4.25 to 4.25
- centres: float32 [4096, 1024], P('comp'), may hold values from -1 to 1
- variances: float32 [4096, 1024], P('comp'), may hold values from 0.15 to 2
- mix_logits: float32 [4096], P('comp'), may hold values from -2 to 2
Outputs:
- new_centres: float32 [4096, 1024], P('comp')
- new_variances: float32 [4096, 1024], P('comp')
- log_weights: float32 [4096], P('comp')
- log_likelihood: float32 [1024], P('dp')
The draws below stay inside these ranges and needn't reach their ends.
All inputs are finite; a program needn't handle non-finite values.
Results may differ from the reference program's by a relative error of at most 0.0014.
Values sent between devices are 32-bit elements; how exact they have to be, the bound alone decides.
A program may use at most 128 MiB of HBM per device.

```python
import math
import jax
import jax.numpy as jnp
from jax import lax

D = 1024
ITERS = 2
POINTS = 1024
K = 4096


def draw_points(key, part):
    inner = jax.random.fold_in(key, 101)
    values = 0.7071 * jax.random.truncated_normal(inner, -6.0, 6.0, (POINTS, D), jnp.float32)
    return values


def draw_centres(key, part):
    base_key, jitter_key = jax.random.split(jax.random.fold_in(key, 211))
    spread = 0.64 / math.sqrt(D)
    base = 0.2 * jax.random.truncated_normal(base_key, -3.0, 3.0, (1, D), jnp.float32)
    jitter = spread * jax.random.truncated_normal(jitter_key, -4.0, 4.0, (K, D), jnp.float32)
    return base + jitter


def draw_variances(key, part):
    base_key, jitter_key = jax.random.split(jax.random.fold_in(key, 307))
    spread = 1.8 / math.sqrt(D)
    low, high = (0.3, 1.0)
    base = jnp.exp(jax.random.uniform(base_key, (1, D), jnp.float32, math.log(low), math.log(high)))
    jitter = jax.random.uniform(jitter_key, (K, D), jnp.float32, -1.7320508, 1.7320508)
    return base * jnp.exp(spread * jitter)


def levels(stream_key, dims, shards, smallest, largest):
    def one(position, blocks):
        heights = jax.random.uniform(jax.random.fold_in(jax.random.fold_in(stream_key, 6), position), (blocks,), jnp.float32, smallest / len(shards), largest / len(shards))
        return jnp.repeat(jnp.exp(heights), dims[position] // blocks).reshape((-1,) + (1,) * (len(dims) - position - 1))

    level = one(*shards[0])
    for cut in shards[1:]:
        level = level * one(*cut)
    return level


def setup_inputs(seed: int = 0) -> dict:
    splits = jax.random.split(jax.random.key(seed), 5)
    return {
        "points": draw_points(jax.random.fold_in(splits[4], 71), 0),
        "centres": draw_centres(jax.random.fold_in(splits[4], 71), 0),
        "variances": draw_variances(jax.random.fold_in(splits[4], 71), 0),
        "mix_logits": jnp.clip(jax.random.uniform(splits[3], (K,), jnp.float32, -2.0, 2.0) * levels(splits[3], (K,), ((0, 4),), -0.4, 0.0), -2.0, 2.0),
    }


LOG_TWO_PI = math.log(2.0 * math.pi)


def contract_rows(left, right):
    return lax.dot_general(left, right, (((1,), (1,)), ((), ())), precision=lax.Precision.HIGHEST, preferred_element_type=jnp.float32)


def contract_points(shares, values):
    return lax.dot_general(shares, values, (((0,), (0,)), ((), ())), precision=lax.Precision.HIGHEST, preferred_element_type=jnp.float32)


def expect(points, squares, centres, variances, mix_logits):
    inverse = 1.0 / variances
    scaled = centres * inverse
    offset = jnp.sum(centres * scaled, 1) + jnp.sum(jnp.log(variances), 1) + points.shape[1] * LOG_TWO_PI
    quadratic = contract_rows(squares, inverse) - 2.0 * contract_rows(points, scaled)
    return mix_logits[None, :] - 0.5 * (quadratic + offset[None, :])


def update(counts, first, second, denominator):
    plus_one = (counts + 1.0)[:, None]
    centre_new = first / plus_one
    spread_new = (second - 2.0 * centre_new * first + plus_one * centre_new * centre_new + 1.0) / (counts + 2.0)[:, None]
    logit_new = jnp.log((counts + 1.0) / denominator)
    return centre_new, spread_new, logit_new


def reference(points, centres, variances, mix_logits):
    squares = points * points
    denominator = jnp.float32(points.shape[0] + centres.shape[0])
    log_norm = jnp.zeros((points.shape[0],), jnp.float32)
    for iteration in range(ITERS):
        density = expect(points, squares, centres, variances, mix_logits)
        highest = jnp.max(density, 1)
        summed = jnp.sum(jnp.exp(density - highest[:, None]), 1)
        log_norm = highest + jnp.log(summed)
        shares = jnp.exp(density - log_norm[:, None])
        counts = jnp.sum(shares, 0)
        first = contract_points(shares, points)
        second = contract_points(shares, squares)
        centres, variances, mix_logits = update(counts, first, second, denominator)
    return centres, variances, mix_logits, log_norm
```

```python
import math

import jax
import jax.numpy as jnp
from jax import lax
from jax.sharding import PartitionSpec as P

ITERS = 2

LOG_TWO_PI = math.log(2.0 * math.pi)


def dot(left, right, contract):
    return lax.dot_general(
        left,
        right,
        (contract, ((), ())),
        precision=lax.Precision.HIGH,
        preferred_element_type=jnp.float32,
    )


def on_device(points, centres, variances, mix_logits):
    width = points.shape[1]
    every = lax.all_gather(points, "dp", axis=0, tiled=True)
    both = jnp.concatenate([every * every, every], 1)
    mine = lax.axis_index("dp") * points.shape[0]
    total = jnp.float32(every.shape[0] + centres.shape[0] * lax.axis_size("comp"))
    log_norm = None
    for iteration in range(ITERS):
        inverse = 1.0 / variances
        scaled = centres * inverse
        offset = jnp.sum(centres * scaled, 1) + jnp.sum(jnp.log(variances), 1) + width * LOG_TWO_PI
        quadratic = dot(jnp.concatenate([inverse, -2.0 * scaled], 1), both, ((1,), (1,)))
        density = (mix_logits - 0.5 * offset)[:, None] - 0.5 * quadratic
        highest = jnp.max(density, 0)
        summed = jnp.sum(jnp.exp(density - highest[None, :]), 0)
        parts = lax.all_gather(jnp.stack([highest, summed]), "comp", axis=0)
        peak = jnp.max(parts[:, 0], 0)
        log_norm = peak + jnp.log(jnp.sum(parts[:, 1] * jnp.exp(parts[:, 0] - peak), 0))
        shares = jnp.exp(density - log_norm[None, :])
        counts = jnp.sum(shares, 1)
        moments = dot(shares, both, ((1,), (0,)))
        second, first = moments[:, :width], moments[:, width:]
        plus_one = (counts + 1.0)[:, None]
        centres = first / plus_one
        variances = (second - 2.0 * centres * first + plus_one * centres * centres + 1.0) / (
            counts + 2.0
        )[:, None]
        mix_logits = jnp.log((counts + 1.0) / total)
    log_norm = lax.dynamic_slice_in_dim(log_norm, mine, points.shape[0], 0)
    return (centres, variances, mix_logits, log_norm)


def solution(mesh):
    return jax.shard_map(
        on_device,
        mesh=mesh,
        in_specs=(P("dp", None), P("comp", None), P("comp", None), P("comp")),
        out_specs=(P("comp", None), P("comp", None), P("comp"), P("dp")),
        check_vma=False,
    )
```

```python
import functools
import math

import jax
import jax.numpy as jnp
from jax import lax
from jax.experimental import pallas as pl
from jax.experimental.pallas import tpu as pltpu
from jax.sharding import PartitionSpec as P

ITERS = 2

LOG_TWO_PI = math.log(2.0 * math.pi)

VMEM_BYTES = 60 * 2**20
TILE = 256


def dot(left, right, contract):
    return lax.dot_general(
        left,
        right,
        (contract, ((), ())),
        precision=lax.Precision.HIGH,
        preferred_element_type=jnp.float32,
    )


def on_device(points, centres, variances, mix_logits):
    width = points.shape[1]
    every = lax.all_gather(points, "dp", axis=0, tiled=True)
    both = jnp.concatenate([every * every, every], 1)
    mine = lax.axis_index("dp") * points.shape[0]
    total = jnp.float32(every.shape[0] + centres.shape[0] * lax.axis_size("comp"))
    log_norm = None
    for iteration in range(ITERS):
        inverse = 1.0 / variances
        scaled = centres * inverse
        offset = jnp.sum(centres * scaled, 1) + jnp.sum(jnp.log(variances), 1) + width * LOG_TWO_PI
        quadratic = dot(jnp.concatenate([inverse, -2.0 * scaled], 1), both, ((1,), (1,)))
        density = (mix_logits - 0.5 * offset)[:, None] - 0.5 * quadratic
        highest = jnp.max(density, 0)
        summed = jnp.sum(jnp.exp(density - highest[None, :]), 0)
        parts = lax.all_gather(jnp.stack([highest, summed]), "comp", axis=0)
        peak = jnp.max(parts[:, 0], 0)
        log_norm = peak + jnp.log(jnp.sum(parts[:, 1] * jnp.exp(parts[:, 0] - peak), 0))
        shares = jnp.exp(density - log_norm[None, :])
        counts = jnp.sum(shares, 1)
        moments = dot(shares, both, ((1,), (0,)))
        second, first = moments[:, :width], moments[:, width:]
        plus_one = (counts + 1.0)[:, None]
        centres = first / plus_one
        variances = (second - 2.0 * centres * first + plus_one * centres * centres + 1.0) / (
            counts + 2.0
        )[:, None]
        mix_logits = jnp.log((counts + 1.0) / total)
    log_norm = lax.dynamic_slice_in_dim(log_norm, mine, points.shape[0], 0)
    return (centres, variances, mix_logits, log_norm)


def split(value):
    high = value.astype(jnp.bfloat16)
    return high, (value - high.astype(jnp.float32)).astype(jnp.bfloat16)


def mm(left, right, contract):
    return lax.dot_general(
        left, right, (contract, ((), ())), preferred_element_type=jnp.float32
    )


NT = ((1,), (1,))
NN = ((1,), (0,))


def shares_of(density, log_norm, rows):
    groups = density.shape[0]
    return jnp.concatenate(
        [jnp.exp(density[g, rows, :] - log_norm[g]) for g in range(groups)], 1
    )


def m_step(shares, right_high, right_low, cols, width, counts):
    high, low = split(shares)

    def moment(at):
        rh = right_high[:, at]
        return mm(high, rh, NN) + (mm(high, right_low[:, at], NN) + mm(low, rh, NN))

    second = moment(pl.ds(cols.start, cols.size))
    first = moment(pl.ds(width + cols.start, cols.size))
    plus_one = counts + 1.0
    centre = first / plus_one
    var = (second - 2.0 * centre * first + plus_one * centre * centre + 1.0) / (counts + 2.0)
    return centre, var


CHUNK = 256


def left_of(centre, var, rows, start, width, left_high, left_low):
    inverse = 1.0 / var
    scaled = centre * inverse
    size = centre.shape[1]
    h, l = split(inverse)
    left_high[rows, pl.ds(start, size)] = h
    left_low[rows, pl.ds(start, size)] = l
    h, l = split(-2.0 * scaled)
    left_high[rows, pl.ds(width + start, size)] = h
    left_low[rows, pl.ds(width + start, size)] = l
    return jnp.sum(centre * scaled + jnp.log(var), 1, keepdims=True)


def em_kernel(
    dp,
    comp,
    points,
    centres_hbm,
    variances_hbm,
    logits,
    density_out,
    right_high_out,
    right_low_out,
    norm_out,
    buf,
    cbuf,
    vbuf,
    left_high,
    left_low,
    right_high,
    right_low,
    density,
    base,
    norm,
    stats,
    local_sem,
    sems,
    stat_sem,
):
    me = lax.axis_index("dp")
    ce = lax.axis_index("comp")
    groups = dp // 2
    z, x = me // 2, me % 2
    half = ce % 2
    rows_here, width = points.shape
    comps = cbuf.shape[0]
    pair = 2 * rows_here
    total = jnp.float32(dp * rows_here + comps * comp)
    mine = pl.ds(pl.multiple_of(half * (width // 2), 128), width // 2)
    other = pl.ds(pl.multiple_of((1 - half) * (width // 2), 128), width // 2)
    partner = {"dp": me, "comp": ce + 1 - 2 * half}
    across = {"dp": me + 1 - 2 * x, "comp": ce}

    loads = [
        pltpu.make_async_copy(points, buf.at[z, pl.ds(x * rows_here, rows_here)], local_sem.at[0]),
        pltpu.make_async_copy(variances_hbm, vbuf, local_sem.at[1]),
        pltpu.make_async_copy(centres_hbm, cbuf, local_sem.at[2]),
    ]
    for load in loads:
        load.start()

    barrier = pltpu.get_barrier_semaphore()
    for hop in range(1, comp):
        pl.semaphore_signal(
            barrier, inc=1, device_id={"dp": me, "comp": lax.rem(ce + hop, comp)}
        )
    pl.semaphore_signal(barrier, inc=1, device_id=across)

    if groups > 1:
        for step in (2, dp - 2):
            pl.semaphore_signal(
                barrier, inc=1, device_id={"dp": lax.rem(me + step, dp), "comp": ce}
            )
    pl.semaphore_wait(barrier, comp + (2 if groups > 1 else 0))

    def copy(block, cols, send, recv, device):
        at = buf.at[block // 2, pl.ds((block % 2) * rows_here, rows_here), cols]
        return pltpu.make_async_remote_copy(
            src_ref=at,
            dst_ref=at,
            send_sem=sems.at[send, block],
            recv_sem=sems.at[recv, block],
            device_id=device,
            device_id_type=pl.DeviceIdType.MESH,
        )

    def up(block):
        return copy(block, mine, 0, 4, {"dp": lax.rem(me + 2, dp), "comp": ce})

    def down(block):
        return copy(block, mine, 1, 4, {"dp": lax.rem(me + dp - 2, dp), "comp": ce})

    def cross(block):
        return copy(block, mine, 2, 5, across)

    def core(block):
        return copy(block, mine, 3, 6, partner)

    def core_in(block):
        return copy(block, other, 3, 6, partner)

    loads[0].wait()

    @pl.when(z < groups - 1)
    def _():
        up(me).start()

    @pl.when(z > 0)
    def _():
        down(me).start()

    cross(me).start()

    loads[1].wait()
    loads[2].wait()

    def prepare(t, carry):
        rows = pl.ds(pl.multiple_of(t * TILE, TILE), TILE)
        offset = jnp.zeros((TILE, 1), jnp.float32)
        for c in range(width // CHUNK):
            at = pl.ds(c * CHUNK, CHUNK)
            offset += left_of(
                cbuf[rows, at], vbuf[rows, at], rows, c * CHUNK, width, left_high, left_low
            )
        base[rows, :] = logits[rows, :] - 0.5 * (offset + width * LOG_TWO_PI)
        return carry

    lax.fori_loop(0, comps // TILE, prepare, 0)

    def e_tile(g, t):
        rows = pl.ds(pl.multiple_of(t * TILE, TILE), TILE)
        ns = pl.ds(pl.multiple_of(g * pair, pair), pair)
        lh, ll = left_high[rows, :], left_low[rows, :]
        rh, rl = right_high[ns, :], right_low[ns, :]
        quadratic = mm(lh, rh, NT) + (mm(lh, rl, NT) + mm(ll, rh, NT))
        density[g, rows, :] = base[rows, :] - 0.5 * quadratic

    def stat(turn, g):
        values = density[g]
        peak = jnp.max(values, 0, keepdims=True)
        stats[turn, ce, g, 0:1, :] = peak
        stats[turn, ce, g, 1:2, :] = jnp.sum(jnp.exp(values - peak), 0, keepdims=True)

    def compute(g):
        ns = pl.ds(pl.multiple_of(g * pair, pair), pair)
        for c in range(width // CHUNK):
            value = buf[g, :, pl.ds(c * CHUNK, CHUNK)]
            h, l = split(value * value)
            right_high[ns, pl.ds(c * CHUNK, CHUNK)] = h
            right_low[ns, pl.ds(c * CHUNK, CHUNK)] = l
            h, l = split(value)
            right_high[ns, pl.ds(width + c * CHUNK, CHUNK)] = h
            right_low[ns, pl.ds(width + c * CHUNK, CHUNK)] = l

        def tile(t, carry):
            e_tile(g, t)
            return carry

        lax.fori_loop(0, comps // TILE, tile, 0)
        stat(0, g)

    def ring(r, carry):
        @pl.when(jnp.logical_and(r > 0, z - r >= 0))
        def _():
            block = me - 2 * r
            up(block).wait_recv()

            @pl.when(z < groups - 1)
            def _():
                up(block).start()

            cross(block).start()
            core(block).start()

        @pl.when(jnp.logical_and(r > 0, z + r < groups))
        def _():
            block = me + 2 * r
            down(block).wait_recv()

            @pl.when(z > 0)
            def _():
                down(block).start()

            cross(block).start()
            core(block).start()

        def side(s, carry):
            g = z + (2 * s - 1) * (r - 1)
            present = jnp.logical_and(
                jnp.logical_and(g >= 0, g < groups),
                jnp.logical_and(r >= 1, jnp.logical_or(s == 0, r > 1)),
            )

            @pl.when(present)
            def _():
                block = 2 * g + 1 - x
                cross(block).wait_recv()
                core(block).start()

            return carry

        lax.fori_loop(0, 2, side, 0)

        def work(s, carry):
            g = z + (2 * s - 1) * (r - 2)
            present = jnp.logical_and(
                jnp.logical_and(g >= 0, g < groups),
                jnp.logical_and(r >= 2, jnp.logical_or(s == 0, r > 2)),
            )

            @pl.when(present)
            def _():
                @pl.when(r > 2)
                def _():
                    core_in(2 * g + x).wait_recv()

                core_in(2 * g + 1 - x).wait_recv()
                compute(g)

            return carry

        lax.fori_loop(0, 2, work, 0)
        return carry

    lax.fori_loop(0, groups + 2, ring, 0)

    def exchange(turn):
        def to(hop):
            return pltpu.make_async_remote_copy(
                src_ref=stats.at[turn, ce],
                dst_ref=stats.at[turn, ce],
                send_sem=stat_sem.at[turn, 0, hop - 1],
                recv_sem=stat_sem.at[turn, 1, hop - 1],
                device_id={"dp": me, "comp": lax.rem(ce + hop, comp)},
                device_id_type=pl.DeviceIdType.MESH,
            )

        for hop in range(1, comp):
            to(hop).start()
        for hop in range(1, comp):
            to(hop).wait()
        peak = stats[turn, 0, :, 0:1, :]
        for c in range(1, comp):
            peak = jnp.maximum(peak, stats[turn, c, :, 0:1, :])
        summed = jnp.zeros_like(peak)
        for c in range(comp):
            summed += stats[turn, c, :, 1:2, :] * jnp.exp(stats[turn, c, :, 0:1, :] - peak)
        norm[...] = peak + jnp.log(summed)

    exchange(0)

    outs = [
        pltpu.make_async_copy(right_high, right_high_out, local_sem.at[0]),
        pltpu.make_async_copy(right_low, right_low_out, local_sem.at[1]),
    ]
    for out in outs:
        out.start()

    def again(t, carry):
        rows = pl.ds(pl.multiple_of(t * TILE, TILE), TILE)
        shares = shares_of(density, norm, rows)
        counts = jnp.sum(shares, 1, keepdims=True)
        offset = jnp.zeros((TILE, 1), jnp.float32)
        for c in range(width // CHUNK):
            centre, var = m_step(
                shares, right_high, right_low, pl.ds(c * CHUNK, CHUNK), width, counts
            )
            offset += left_of(centre, var, rows, c * CHUNK, width, left_high, left_low)
        logit = jnp.log((counts + 1.0) / total)
        base[rows, :] = logit - 0.5 * (offset + width * LOG_TWO_PI)

        def group(g, carry):
            e_tile(g, t)
            return carry

        lax.fori_loop(0, groups, group, 0)
        return carry

    for turn in range(1, ITERS):
        lax.fori_loop(0, comps // TILE, again, 0)

        def each(g, carry, turn=turn):
            stat(turn, g)
            return carry

        lax.fori_loop(0, groups, each, 0)
        exchange(turn)

    last = pltpu.make_async_copy(density, density_out, local_sem.at[2])
    last.start()
    norm_out[...] = norm[...]

    @pl.when(z < groups - 1)
    def _():
        up(me).wait_send()

    @pl.when(z > 0)
    def _():
        down(me).wait_send()

    cross(me).wait_send()

    def drain(block, carry):
        g = block // 2

        @pl.when(jnp.logical_and(block % 2 == x, g < z))
        def _():
            @pl.when(z < groups - 1)
            def _():
                up(block).wait_send()

            cross(block).wait_send()

        @pl.when(jnp.logical_and(block % 2 == x, g > z))
        def _():
            @pl.when(z > 0)
            def _():
                down(block).wait_send()

            cross(block).wait_send()

        @pl.when(block != me)
        def _():
            core(block).wait_send()

        return carry

    lax.fori_loop(0, dp, drain, 0)
    last.wait()
    for out in outs:
        out.wait()


def last_kernel(total, density, norm, right_high, right_low, centre_out, var_out, logit_out):
    width = centre_out.shape[1]
    shares = shares_of(density, norm, slice(None))
    counts = jnp.sum(shares, 1, keepdims=True)
    for c in range(width // CHUNK):
        at = pl.ds(c * CHUNK, CHUNK)
        centre, var = m_step(shares, right_high, right_low, at, width, counts)
        centre_out[:, at] = centre
        var_out[:, at] = var
    logit_out[...] = jnp.log((counts + 1.0) / total)


def fused(dp, comp, points, centres, variances, mix_logits):
    rows_here, width = points.shape
    comps = centres.shape[0]
    groups, pair, every = dp // 2, 2 * rows_here, dp * rows_here
    f32, bf16 = jnp.float32, jnp.bfloat16
    vmem, anyw = pl.BlockSpec(memory_space=pltpu.VMEM), pl.BlockSpec(memory_space=pl.ANY)
    density, high, low, norm = pl.pallas_call(
        functools.partial(em_kernel, dp, comp),
        out_shape=[
            jax.ShapeDtypeStruct((groups, comps, pair), f32),
            jax.ShapeDtypeStruct((every, 2 * width), bf16),
            jax.ShapeDtypeStruct((every, 2 * width), bf16),
            jax.ShapeDtypeStruct((groups, 1, pair), f32),
        ],
        in_specs=[anyw, anyw, anyw, vmem],
        out_specs=[anyw, anyw, anyw, vmem],
        scratch_shapes=[
            pltpu.VMEM((groups, pair, width), f32),
            pltpu.VMEM((comps, width), f32),
            pltpu.VMEM((comps, width), f32),
            pltpu.VMEM((comps, 2 * width), bf16),
            pltpu.VMEM((comps, 2 * width), bf16),
            pltpu.VMEM((every, 2 * width), bf16),
            pltpu.VMEM((every, 2 * width), bf16),
            pltpu.VMEM((groups, comps, pair), f32),
            pltpu.VMEM((comps, 1), f32),
            pltpu.VMEM((groups, 1, pair), f32),
            pltpu.VMEM((ITERS, comp, groups, 2, pair), f32),
            pltpu.SemaphoreType.DMA((3,)),
            pltpu.SemaphoreType.DMA((7, dp)),
            pltpu.SemaphoreType.DMA((ITERS, 2, comp - 1)),
        ],
        compiler_params=pltpu.CompilerParams(
            collective_id=0, has_side_effects=True, vmem_limit_bytes=VMEM_BYTES
        ),
        name="em",
    )(points, centres, variances, mix_logits[:, None])
    total = float(every + comps * comp)
    whole = lambda *shape: pl.BlockSpec(shape, lambda t: (0,) * len(shape))
    centre, var, logit = pl.pallas_call(
        functools.partial(last_kernel, total),
        grid=(comps // TILE,),
        out_shape=[
            jax.ShapeDtypeStruct((comps, width), f32),
            jax.ShapeDtypeStruct((comps, width), f32),
            jax.ShapeDtypeStruct((comps, 1), f32),
        ],
        in_specs=[
            pl.BlockSpec((groups, TILE, pair), lambda t: (0, t, 0)),
            whole(groups, 1, pair),
            whole(every, 2 * width),
            whole(every, 2 * width),
        ],
        out_specs=[
            pl.BlockSpec((TILE, width), lambda t: (t, 0)),
            pl.BlockSpec((TILE, width), lambda t: (t, 0)),
            pl.BlockSpec((TILE, 1), lambda t: (t, 0)),
        ],
        compiler_params=pltpu.CompilerParams(vmem_limit_bytes=VMEM_BYTES),
        name="last",
    )(density, norm, high, low)
    here = lax.axis_index("dp")
    log_norm = lax.dynamic_slice_in_dim(norm.reshape(every), here * rows_here, rows_here, 0)
    return centre, var, logit[:, 0], log_norm


def solution(mesh):
    dp, comp = mesh.shape["dp"], mesh.shape["comp"]

    def body(points, centres, variances, mix_logits):
        rows, width = points.shape
        comps = centres.shape[0]
        every = dp * rows
        need = every * width * 12 + comps * width * 16 + comps * every * 4
        fits = need < VMEM_BYTES * 3 // 4 and dp % 2 == 0 and comp % 2 == 0
        form = functools.partial(fused, dp, comp) if fits else on_device
        return form(points, centres, variances, mix_logits)

    return jax.shard_map(
        body,
        mesh=mesh,
        in_specs=(P("dp", None), P("comp", None), P("comp", None), P("comp")),
        out_specs=(P("comp", None), P("comp", None), P("comp"), P("dp")),
        check_vma=False,
    )
```

```python
import functools
import math

import jax
import jax.numpy as jnp
from jax import lax
from jax.experimental import pallas as pl
from jax.experimental.pallas import tpu as pltpu
from jax.sharding import PartitionSpec as P

ITERS = 2

LOG_TWO_PI = math.log(2.0 * math.pi)

VMEM_BYTES = 60 * 2**20
TILE = 256


def dot(left, right, contract):
    return lax.dot_general(
        left,
        right,
        (contract, ((), ())),
        precision=lax.Precision.HIGH,
        preferred_element_type=jnp.float32,
    )


def on_device(points, centres, variances, mix_logits):
    width = points.shape[1]
    every = lax.all_gather(points, "dp", axis=0, tiled=True)
    both = jnp.concatenate([every * every, every], 1)
    mine = lax.axis_index("dp") * points.shape[0]
    total = jnp.float32(every.shape[0] + centres.shape[0] * lax.axis_size("comp"))
    log_norm = None
    for iteration in range(ITERS):
        inverse = 1.0 / variances
        scaled = centres * inverse
        offset = jnp.sum(centres * scaled, 1) + jnp.sum(jnp.log(variances), 1) + width * LOG_TWO_PI
        quadratic = dot(jnp.concatenate([inverse, -2.0 * scaled], 1), both, ((1,), (1,)))
        density = (mix_logits - 0.5 * offset)[:, None] - 0.5 * quadratic
        highest = jnp.max(density, 0)
        summed = jnp.sum(jnp.exp(density - highest[None, :]), 0)
        parts = lax.all_gather(jnp.stack([highest, summed]), "comp", axis=0)
        peak = jnp.max(parts[:, 0], 0)
        log_norm = peak + jnp.log(jnp.sum(parts[:, 1] * jnp.exp(parts[:, 0] - peak), 0))
        shares = jnp.exp(density - log_norm[None, :])
        counts = jnp.sum(shares, 1)
        moments = dot(shares, both, ((1,), (0,)))
        second, first = moments[:, :width], moments[:, width:]
        plus_one = (counts + 1.0)[:, None]
        centres = first / plus_one
        variances = (second - 2.0 * centres * first + plus_one * centres * centres + 1.0) / (
            counts + 2.0
        )[:, None]
        mix_logits = jnp.log((counts + 1.0) / total)
    log_norm = lax.dynamic_slice_in_dim(log_norm, mine, points.shape[0], 0)
    return (centres, variances, mix_logits, log_norm)


def split(value):
    high = value.astype(jnp.bfloat16)
    return high, (value - high.astype(jnp.float32)).astype(jnp.bfloat16)


def mm(left, right, contract):
    return lax.dot_general(
        left, right, (contract, ((), ())), preferred_element_type=jnp.float32
    )


NT = ((1,), (1,))
NN = ((1,), (0,))


LANES = 128


def diagonal():
    shape = (LANES, LANES)
    return lax.broadcasted_iota(jnp.int32, shape, 0) == lax.broadcasted_iota(jnp.int32, shape, 1)


def to_column(row):
    keep = diagonal()
    return jnp.concatenate(
        [
            jnp.sum(jnp.where(keep, row[:, c : c + LANES], 0.0), 1, keepdims=True)
            for c in range(0, row.shape[1], LANES)
        ],
        0,
    )


def to_row(column):
    keep = diagonal()
    return jnp.concatenate(
        [
            jnp.sum(jnp.where(keep, column[c : c + LANES, :], 0.0), 0, keepdims=True)
            for c in range(0, column.shape[0], LANES)
        ],
        1,
    )


def shares_of(density, log_norm, rows):
    groups = density.shape[0]
    return jnp.concatenate(
        [jnp.exp(density[g, rows, :] - log_norm[g]) for g in range(groups)], 1
    )


def m_step(high, low, right_high, right_low, cols, width, counts):
    def moment(at):
        rh = right_high[:, at]
        return mm(high, rh, NN) + (mm(high, right_low[:, at], NN) + mm(low, rh, NN))

    second = moment(pl.ds(cols.start, cols.size))
    first = moment(pl.ds(width + cols.start, cols.size))
    plus_one = counts + 1.0
    centre = first / plus_one
    var = (second - 2.0 * centre * first + plus_one * centre * centre + 1.0) / (counts + 2.0)
    return centre, var


CHUNK = 256


def left_of(centre, var, rows, start, width, left_high, left_low):
    inverse = 1.0 / var
    scaled = centre * inverse
    size = centre.shape[1]
    h, l = split(inverse)
    left_high[rows, pl.ds(start, size)] = h
    left_low[rows, pl.ds(start, size)] = l
    h, l = split(-2.0 * scaled)
    left_high[rows, pl.ds(width + start, size)] = h
    left_low[rows, pl.ds(width + start, size)] = l
    return jnp.sum(centre * scaled + jnp.log(var), 1, keepdims=True)


def em_kernel(
    dp,
    comp,
    points,
    centres_hbm,
    variances_hbm,
    logits,
    density_out,
    right_high_out,
    right_low_out,
    norm_out,
    mine_out,
    buf,
    cbuf,
    vbuf,
    left_high,
    left_low,
    right_high,
    right_low,
    density,
    base,
    norm,
    stats,
    local_sem,
    sems,
    stat_sem,
    leave_sem,
):
    me = lax.axis_index("dp")
    ce = lax.axis_index("comp")
    groups = dp // 2
    z, x = me // 2, me % 2
    half = ce % 2
    rows_here, width = points.shape
    comps = cbuf.shape[0]
    pair = 2 * rows_here
    total = jnp.float32(dp * rows_here + comps * comp)
    mine = pl.ds(pl.multiple_of(half * (width // 2), 128), width // 2)
    other = pl.ds(pl.multiple_of((1 - half) * (width // 2), 128), width // 2)
    partner = {"dp": me, "comp": ce + 1 - 2 * half}
    across = {"dp": me + 1 - 2 * x, "comp": ce}

    loads = [
        pltpu.make_async_copy(points, buf.at[z, pl.ds(x * rows_here, rows_here)], local_sem.at[0]),
        pltpu.make_async_copy(variances_hbm, vbuf, local_sem.at[1]),
        pltpu.make_async_copy(centres_hbm, cbuf, local_sem.at[2]),
    ]
    for load in loads:
        load.start()

    barrier = pltpu.get_barrier_semaphore()
    for hop in range(1, comp):
        pl.semaphore_signal(
            barrier, inc=1, device_id={"dp": me, "comp": lax.rem(ce + hop, comp)}
        )
    pl.semaphore_signal(barrier, inc=1, device_id=across)

    if groups > 1:
        for step in (2, dp - 2):
            pl.semaphore_signal(
                barrier, inc=1, device_id={"dp": lax.rem(me + step, dp), "comp": ce}
            )
    pl.semaphore_wait(barrier, comp + (2 if groups > 1 else 0))

    def copy(block, cols, send, recv, device):
        at = buf.at[block // 2, pl.ds((block % 2) * rows_here, rows_here), cols]
        return pltpu.make_async_remote_copy(
            src_ref=at,
            dst_ref=at,
            send_sem=sems.at[send, block],
            recv_sem=sems.at[recv, block],
            device_id=device,
            device_id_type=pl.DeviceIdType.MESH,
        )

    def up(block):
        return copy(block, mine, 0, 4, {"dp": lax.rem(me + 2, dp), "comp": ce})

    def down(block):
        return copy(block, mine, 1, 4, {"dp": lax.rem(me + dp - 2, dp), "comp": ce})

    def cross(block):
        return copy(block, mine, 2, 5, across)

    def core(block):
        return copy(block, mine, 3, 6, partner)

    def core_in(block):
        return copy(block, other, 3, 6, partner)

    loads[0].wait()

    @pl.when(z < groups - 1)
    def _():
        up(me).start()

    @pl.when(z > 0)
    def _():
        down(me).start()

    cross(me).start()

    loads[1].wait()
    loads[2].wait()

    def prepare(t, carry):
        rows = pl.ds(pl.multiple_of(t * TILE, TILE), TILE)
        offset = jnp.zeros((TILE, 1), jnp.float32)
        for c in range(width // CHUNK):
            at = pl.ds(c * CHUNK, CHUNK)
            offset += left_of(
                cbuf[rows, at], vbuf[rows, at], rows, c * CHUNK, width, left_high, left_low
            )
        base[rows, :] = to_column(logits[:, rows]) - 0.5 * (offset + width * LOG_TWO_PI)
        return carry

    lax.fori_loop(0, comps // TILE, prepare, 0)

    def e_tile(g, t):
        rows = pl.ds(pl.multiple_of(t * TILE, TILE), TILE)
        ns = pl.ds(pl.multiple_of(g * pair, pair), pair)
        lh, ll = left_high[rows, :], left_low[rows, :]
        rh, rl = right_high[ns, :], right_low[ns, :]
        quadratic = mm(lh, rh, NT) + (mm(lh, rl, NT) + mm(ll, rh, NT))
        density[g, rows, :] = base[rows, :] - 0.5 * quadratic

    def stat(turn, g):
        values = density[g]
        peak = jnp.max(values, 0, keepdims=True)
        stats[turn, ce, g, 0:1, :] = peak
        stats[turn, ce, g, 1:2, :] = jnp.sum(jnp.exp(values - peak), 0, keepdims=True)

    def compute(g):
        ns = pl.ds(pl.multiple_of(g * pair, pair), pair)
        for c in range(width // CHUNK):
            value = buf[g, :, pl.ds(c * CHUNK, CHUNK)]
            h, l = split(value * value)
            right_high[ns, pl.ds(c * CHUNK, CHUNK)] = h
            right_low[ns, pl.ds(c * CHUNK, CHUNK)] = l
            h, l = split(value)
            right_high[ns, pl.ds(width + c * CHUNK, CHUNK)] = h
            right_low[ns, pl.ds(width + c * CHUNK, CHUNK)] = l

        def tile(t, carry):
            e_tile(g, t)
            return carry

        lax.fori_loop(0, comps // TILE, tile, 0)
        stat(0, g)

    def ring(r, carry):
        @pl.when(jnp.logical_and(r > 0, z - r >= 0))
        def _():
            block = me - 2 * r
            up(block).wait_recv()

            @pl.when(z < groups - 1)
            def _():
                up(block).start()

            cross(block).start()
            core(block).start()

        @pl.when(jnp.logical_and(r > 0, z + r < groups))
        def _():
            block = me + 2 * r
            down(block).wait_recv()

            @pl.when(z > 0)
            def _():
                down(block).start()

            cross(block).start()
            core(block).start()

        def side(s, carry):
            g = z + (2 * s - 1) * (r - 1)
            present = jnp.logical_and(
                jnp.logical_and(g >= 0, g < groups),
                jnp.logical_and(r >= 1, jnp.logical_or(s == 0, r > 1)),
            )

            @pl.when(present)
            def _():
                block = 2 * g + 1 - x
                cross(block).wait_recv()
                core(block).start()

            return carry

        lax.fori_loop(0, 2, side, 0)

        def work(s, carry):
            g = z + (2 * s - 1) * (r - 2)
            present = jnp.logical_and(
                jnp.logical_and(g >= 0, g < groups),
                jnp.logical_and(r >= 2, jnp.logical_or(s == 0, r > 2)),
            )

            @pl.when(present)
            def _():
                @pl.when(r > 2)
                def _():
                    core_in(2 * g + x).wait_recv()

                core_in(2 * g + 1 - x).wait_recv()
                compute(g)

            return carry

        lax.fori_loop(0, 2, work, 0)
        return carry

    lax.fori_loop(0, groups + 2, ring, 0)

    def exchange(turn):
        def to(hop):
            return pltpu.make_async_remote_copy(
                src_ref=stats.at[turn, ce],
                dst_ref=stats.at[turn, ce],
                send_sem=stat_sem.at[turn, 0, hop - 1],
                recv_sem=stat_sem.at[turn, 1, hop - 1],
                device_id={"dp": me, "comp": lax.rem(ce + hop, comp)},
                device_id_type=pl.DeviceIdType.MESH,
            )

        for hop in range(1, comp):
            to(hop).start()
        for hop in range(1, comp):
            to(hop).wait()
        peak = stats[turn, 0, :, 0:1, :]
        for c in range(1, comp):
            peak = jnp.maximum(peak, stats[turn, c, :, 0:1, :])
        summed = jnp.zeros_like(peak)
        for c in range(comp):
            summed += stats[turn, c, :, 1:2, :] * jnp.exp(stats[turn, c, :, 0:1, :] - peak)
        norm[...] = peak + jnp.log(summed)

    exchange(0)

    outs = [
        pltpu.make_async_copy(right_high, right_high_out, local_sem.at[0]),
        pltpu.make_async_copy(right_low, right_low_out, local_sem.at[1]),
    ]
    for out in outs:
        out.start()

    def leave(t):
        rows = pl.ds(pl.multiple_of(t * TILE, TILE), TILE)
        return pltpu.make_async_copy(
            density.at[:, rows, :], density_out.at[:, rows, :], leave_sem.at[t]
        )

    def again(turn, t, carry):
        rows = pl.ds(pl.multiple_of(t * TILE, TILE), TILE)
        shares = shares_of(density, norm, rows)
        counts = jnp.sum(shares, 1, keepdims=True)
        high, low = split(shares)
        offset = jnp.zeros((TILE, 1), jnp.float32)
        for c in range(width // CHUNK):
            centre, var = m_step(
                high, low, right_high, right_low, pl.ds(c * CHUNK, CHUNK), width, counts
            )
            offset += left_of(centre, var, rows, c * CHUNK, width, left_high, left_low)
        logit = jnp.log((counts + 1.0) / total)
        base[rows, :] = logit - 0.5 * (offset + width * LOG_TWO_PI)

        def group(g, carry):
            e_tile(g, t)
            return carry

        lax.fori_loop(0, groups, group, 0)
        if turn == ITERS - 1:
            leave(t).start()
        return carry

    for turn in range(1, ITERS):
        lax.fori_loop(0, comps // TILE, functools.partial(again, turn), 0)

        def each(g, carry, turn=turn):
            stat(turn, g)
            return carry

        lax.fori_loop(0, groups, each, 0)
        exchange(turn)

    norm_out[...] = norm[...]
    lanes = pl.ds(pl.multiple_of(x * rows_here, LANES), rows_here)
    mine_out[...] = norm[z, :, lanes]

    @pl.when(z < groups - 1)
    def _():
        up(me).wait_send()

    @pl.when(z > 0)
    def _():
        down(me).wait_send()

    cross(me).wait_send()

    def drain(block, carry):
        g = block // 2

        @pl.when(jnp.logical_and(block % 2 == x, g < z))
        def _():
            @pl.when(z < groups - 1)
            def _():
                up(block).wait_send()

            cross(block).wait_send()

        @pl.when(jnp.logical_and(block % 2 == x, g > z))
        def _():
            @pl.when(z > 0)
            def _():
                down(block).wait_send()

            cross(block).wait_send()

        @pl.when(block != me)
        def _():
            core(block).wait_send()

        return carry

    lax.fori_loop(0, dp, drain, 0)

    def left(t, carry):
        leave(t).wait()
        return carry

    lax.fori_loop(0, comps // TILE, left, 0)
    for out in outs:
        out.wait()


def last_kernel(
    total,
    density,
    norm,
    right_high,
    right_low,
    mine,
    centre_out,
    var_out,
    logit_out,
    mine_out,
):
    width = centre_out.shape[1]
    shares = shares_of(density, norm, slice(None))
    counts = jnp.sum(shares, 1, keepdims=True)
    high, low = split(shares)
    for c in range(width // CHUNK):
        at = pl.ds(c * CHUNK, CHUNK)
        centre, var = m_step(high, low, right_high, right_low, at, width, counts)
        centre_out[:, at] = centre
        var_out[:, at] = var
    logit_out[...] = to_row(jnp.log((counts + 1.0) / total))
    mine_out[...] = mine[...]


def fused(dp, comp, points, centres, variances, mix_logits):
    rows_here, width = points.shape
    comps = centres.shape[0]
    groups, pair, every = dp // 2, 2 * rows_here, dp * rows_here
    f32, bf16 = jnp.float32, jnp.bfloat16
    vmem, anyw = pl.BlockSpec(memory_space=pltpu.VMEM), pl.BlockSpec(memory_space=pl.ANY)
    density, high, low, norm, mine = pl.pallas_call(
        functools.partial(em_kernel, dp, comp),
        out_shape=[
            jax.ShapeDtypeStruct((groups, comps, pair), f32),
            jax.ShapeDtypeStruct((every, 2 * width), bf16),
            jax.ShapeDtypeStruct((every, 2 * width), bf16),
            jax.ShapeDtypeStruct((groups, 1, pair), f32),
            jax.ShapeDtypeStruct((1, rows_here), f32),
        ],
        in_specs=[anyw, anyw, anyw, vmem],
        out_specs=[anyw, anyw, anyw, vmem, vmem],
        scratch_shapes=[
            pltpu.VMEM((groups, pair, width), f32),
            pltpu.VMEM((comps, width), f32),
            pltpu.VMEM((comps, width), f32),
            pltpu.VMEM((comps, 2 * width), bf16),
            pltpu.VMEM((comps, 2 * width), bf16),
            pltpu.VMEM((every, 2 * width), bf16),
            pltpu.VMEM((every, 2 * width), bf16),
            pltpu.VMEM((groups, comps, pair), f32),
            pltpu.VMEM((comps, 1), f32),
            pltpu.VMEM((groups, 1, pair), f32),
            pltpu.VMEM((ITERS, comp, groups, 2, pair), f32),
            pltpu.SemaphoreType.DMA((3,)),
            pltpu.SemaphoreType.DMA((7, dp)),
            pltpu.SemaphoreType.DMA((ITERS, 2, comp - 1)),
            pltpu.SemaphoreType.DMA((comps // TILE,)),
        ],
        compiler_params=pltpu.CompilerParams(
            collective_id=0, has_side_effects=True, vmem_limit_bytes=VMEM_BYTES
        ),
        name="em",
    )(points, centres, variances, mix_logits[None, :])
    total = float(every + comps * comp)
    whole = lambda *shape: pl.BlockSpec(shape, lambda t: (0,) * len(shape))
    centre, var, logit, log_norm = pl.pallas_call(
        functools.partial(last_kernel, total),
        grid=(comps // TILE,),
        out_shape=[
            jax.ShapeDtypeStruct((comps, width), f32),
            jax.ShapeDtypeStruct((comps, width), f32),
            jax.ShapeDtypeStruct((1, comps), f32),
            jax.ShapeDtypeStruct((1, rows_here), f32),
        ],
        in_specs=[
            pl.BlockSpec((groups, TILE, pair), lambda t: (0, t, 0)),
            whole(groups, 1, pair),
            whole(every, 2 * width),
            whole(every, 2 * width),
            whole(1, rows_here),
        ],
        out_specs=[
            pl.BlockSpec((TILE, width), lambda t: (t, 0)),
            pl.BlockSpec((TILE, width), lambda t: (t, 0)),
            pl.BlockSpec((1, TILE), lambda t: (0, t)),
            whole(1, rows_here),
        ],
        compiler_params=pltpu.CompilerParams(vmem_limit_bytes=VMEM_BYTES),
        name="last",
    )(density, norm, high, low, mine)
    return centre, var, logit.reshape(comps), log_norm.reshape(rows_here)


def solution(mesh):
    dp, comp = mesh.shape["dp"], mesh.shape["comp"]

    def body(points, centres, variances, mix_logits):
        rows, width = points.shape
        comps = centres.shape[0]
        every = dp * rows
        need = every * width * 12 + comps * width * 16 + comps * every * 4
        fits = need < VMEM_BYTES * 3 // 4 and dp % 2 == 0 and comp % 2 == 0
        fits = fits and rows % LANES == 0 and comps % TILE == 0
        form = functools.partial(fused, dp, comp) if fits else on_device
        return form(points, centres, variances, mix_logits)

    return jax.shard_map(
        body,
        mesh=mesh,
        in_specs=(P("dp", None), P("comp", None), P("comp", None), P("comp")),
        out_specs=(P("comp", None), P("comp", None), P("comp"), P("dp")),
        check_vma=False,
    )
```

```python
import functools
import math

import jax
import jax.numpy as jnp
from jax import lax
from jax.experimental import pallas as pl
from jax.experimental.pallas import tpu as pltpu
from jax.sharding import PartitionSpec as P

ITERS = 2

LOG_TWO_PI = math.log(2.0 * math.pi)

VMEM_BYTES = 60 * 2**20
TILE = 256


def dot(left, right, contract):
    return lax.dot_general(
        left,
        right,
        (contract, ((), ())),
        precision=lax.Precision.HIGH,
        preferred_element_type=jnp.float32,
    )


def on_device(points, centres, variances, mix_logits):
    width = points.shape[1]
    every = lax.all_gather(points, "dp", axis=0, tiled=True)
    both = jnp.concatenate([every * every, every], 1)
    mine = lax.axis_index("dp") * points.shape[0]
    total = jnp.float32(every.shape[0] + centres.shape[0] * lax.axis_size("comp"))
    log_norm = None
    for iteration in range(ITERS):
        inverse = 1.0 / variances
        scaled = centres * inverse
        offset = jnp.sum(centres * scaled, 1) + jnp.sum(jnp.log(variances), 1) + width * LOG_TWO_PI
        quadratic = dot(jnp.concatenate([inverse, -2.0 * scaled], 1), both, ((1,), (1,)))
        density = (mix_logits - 0.5 * offset)[:, None] - 0.5 * quadratic
        highest = jnp.max(density, 0)
        summed = jnp.sum(jnp.exp(density - highest[None, :]), 0)
        parts = lax.all_gather(jnp.stack([highest, summed]), "comp", axis=0)
        peak = jnp.max(parts[:, 0], 0)
        log_norm = peak + jnp.log(jnp.sum(parts[:, 1] * jnp.exp(parts[:, 0] - peak), 0))
        shares = jnp.exp(density - log_norm[None, :])
        counts = jnp.sum(shares, 1)
        moments = dot(shares, both, ((1,), (0,)))
        second, first = moments[:, :width], moments[:, width:]
        plus_one = (counts + 1.0)[:, None]
        centres = first / plus_one
        variances = (second - 2.0 * centres * first + plus_one * centres * centres + 1.0) / (
            counts + 2.0
        )[:, None]
        mix_logits = jnp.log((counts + 1.0) / total)
    log_norm = lax.dynamic_slice_in_dim(log_norm, mine, points.shape[0], 0)
    return (centres, variances, mix_logits, log_norm)


def split(value):
    high = value.astype(jnp.bfloat16)
    return high, (value - high.astype(jnp.float32)).astype(jnp.bfloat16)


def mm(left, right, contract):
    return lax.dot_general(
        left, right, (contract, ((), ())), preferred_element_type=jnp.float32
    )


NT = ((1,), (1,))
NN = ((1,), (0,))


LANES = 128


def diagonal():
    shape = (LANES, LANES)
    return lax.broadcasted_iota(jnp.int32, shape, 0) == lax.broadcasted_iota(jnp.int32, shape, 1)


def to_column(row):
    keep = diagonal()
    return jnp.concatenate(
        [
            jnp.sum(jnp.where(keep, row[:, c : c + LANES], 0.0), 1, keepdims=True)
            for c in range(0, row.shape[1], LANES)
        ],
        0,
    )


def to_row(column):
    keep = diagonal()
    return jnp.concatenate(
        [
            jnp.sum(jnp.where(keep, column[c : c + LANES, :], 0.0), 0, keepdims=True)
            for c in range(0, column.shape[0], LANES)
        ],
        1,
    )


def shares_of(density, log_norm, rows):
    groups = density.shape[0]
    return jnp.concatenate(
        [jnp.exp(density[g, rows, :] - log_norm[g]) for g in range(groups)], 1
    )


def m_step(high, low, right_high, right_low, cols, width, counts):
    def moment(at):
        rh = right_high[:, at]
        return mm(high, rh, NN) + (mm(high, right_low[:, at], NN) + mm(low, rh, NN))

    second = moment(pl.ds(cols.start, cols.size))
    first = moment(pl.ds(width + cols.start, cols.size))
    plus_one = counts + 1.0
    centre = first / plus_one
    var = (second - 2.0 * centre * first + plus_one * centre * centre + 1.0) / (counts + 2.0)
    return centre, var


CHUNK = 256


def left_of(centre, var, rows, start, width, left_high, left_low):
    inverse = 1.0 / var
    scaled = centre * inverse
    size = centre.shape[1]
    h, l = split(inverse)
    left_high[rows, pl.ds(start, size)] = h
    left_low[rows, pl.ds(start, size)] = l
    h, l = split(-2.0 * scaled)
    left_high[rows, pl.ds(width + start, size)] = h
    left_low[rows, pl.ds(width + start, size)] = l
    return jnp.sum(centre * scaled + jnp.log(var), 1, keepdims=True)


def em_kernel(
    dp,
    comp,
    points,
    centres_hbm,
    variances_hbm,
    logits,
    density_out,
    right_high_out,
    right_low_out,
    norm_out,
    mine_out,
    buf,
    cbuf,
    vbuf,
    left_high,
    left_low,
    right_high,
    right_low,
    density,
    base,
    norm,
    stats,
    local_sem,
    sems,
    stat_sem,
    leave_sem,
):
    me = lax.axis_index("dp")
    ce = lax.axis_index("comp")
    groups = dp // 2
    z, x = me // 2, me % 2
    half = ce % 2
    rows_here, width = points.shape
    comps = cbuf.shape[0]
    pair = 2 * rows_here
    total = jnp.float32(dp * rows_here + comps * comp)
    y = (ce // 2) % 2

    def cols_of(h, q, parts):
        start = h * (width // 2) + q * (width // 4)
        return pl.ds(pl.multiple_of(start, LANES), width // parts)

    mine, other = cols_of(half, 0, 2), cols_of(1 - half, 0, 2)
    mine_near, mine_far = cols_of(half, y, 4), cols_of(half, 1 - y, 4)
    other_near, other_far = cols_of(1 - half, y, 4), cols_of(1 - half, 1 - y, 4)
    partner = {"dp": me, "comp": ce + 1 - 2 * half}
    beside = {"dp": me, "comp": ce + 2 - 4 * y}
    across = {"dp": me + 1 - 2 * x, "comp": ce}

    loads = [
        pltpu.make_async_copy(points, buf.at[z, pl.ds(x * rows_here, rows_here)], local_sem.at[0]),
        pltpu.make_async_copy(variances_hbm, vbuf, local_sem.at[1]),
        pltpu.make_async_copy(centres_hbm, cbuf, local_sem.at[2]),
    ]
    for load in loads:
        load.start()

    barrier = pltpu.get_barrier_semaphore()
    for hop in range(1, comp):
        pl.semaphore_signal(
            barrier, inc=1, device_id={"dp": me, "comp": lax.rem(ce + hop, comp)}
        )
    pl.semaphore_signal(barrier, inc=1, device_id=across)

    if groups > 1:
        for step in (2, dp - 2):
            pl.semaphore_signal(
                barrier, inc=1, device_id={"dp": lax.rem(me + step, dp), "comp": ce}
            )
    pl.semaphore_wait(barrier, comp + (2 if groups > 1 else 0))

    def copy(block, cols, send, recv, device):
        at = buf.at[block // 2, pl.ds((block % 2) * rows_here, rows_here), cols]
        return pltpu.make_async_remote_copy(
            src_ref=at,
            dst_ref=at,
            send_sem=sems.at[send, block],
            recv_sem=sems.at[recv, block],
            device_id=device,
            device_id_type=pl.DeviceIdType.MESH,
        )

    def up(block):
        return copy(block, mine, 0, 4, {"dp": lax.rem(me + 2, dp), "comp": ce})

    def down(block):
        return copy(block, mine, 1, 4, {"dp": lax.rem(me + dp - 2, dp), "comp": ce})

    def cross(block):
        return copy(block, mine_near, 2, 5, across)

    def side(block, cols):
        return copy(block, cols, 7, 8, beside)

    def core(block, cols):
        return copy(block, cols, 3, 6, partner)

    def core_far(block, cols):
        return copy(block, cols, 9, 10, partner)

    loads[0].wait()

    @pl.when(z < groups - 1)
    def _():
        up(me).start()

    @pl.when(z > 0)
    def _():
        down(me).start()

    cross(me).start()

    def prepare(t, carry):
        rows = pl.ds(pl.multiple_of(t * TILE, TILE), TILE)
        offset = jnp.zeros((TILE, 1), jnp.float32)
        for c in range(width // CHUNK):
            at = pl.ds(c * CHUNK, CHUNK)
            offset += left_of(
                cbuf[rows, at], vbuf[rows, at], rows, c * CHUNK, width, left_high, left_low
            )
        base[rows, :] = to_column(logits[:, rows]) - 0.5 * (offset + width * LOG_TWO_PI)
        return carry

    def e_tile(g, t):
        rows = pl.ds(pl.multiple_of(t * TILE, TILE), TILE)
        ns = pl.ds(pl.multiple_of(g * pair, pair), pair)
        lh, ll = left_high[rows, :], left_low[rows, :]
        rh, rl = right_high[ns, :], right_low[ns, :]
        quadratic = mm(lh, rh, NT) + (mm(lh, rl, NT) + mm(ll, rh, NT))
        density[g, rows, :] = base[rows, :] - 0.5 * quadratic

    def stat(turn, g):
        values = density[g]
        peak = jnp.max(values, 0, keepdims=True)
        stats[turn, ce, g, 0:1, :] = peak
        stats[turn, ce, g, 1:2, :] = jnp.sum(jnp.exp(values - peak), 0, keepdims=True)

    def compute(g):
        ns = pl.ds(pl.multiple_of(g * pair, pair), pair)
        for c in range(width // CHUNK):
            value = buf[g, :, pl.ds(c * CHUNK, CHUNK)]
            h, l = split(value * value)
            right_high[ns, pl.ds(c * CHUNK, CHUNK)] = h
            right_low[ns, pl.ds(c * CHUNK, CHUNK)] = l
            h, l = split(value)
            right_high[ns, pl.ds(width + c * CHUNK, CHUNK)] = h
            right_low[ns, pl.ds(width + c * CHUNK, CHUNK)] = l

        def tile(t, carry):
            e_tile(g, t)
            return carry

        lax.fori_loop(0, comps // TILE, tile, 0)
        stat(0, g)

    def line(r):
        @pl.when(z - r >= 0)
        def _():
            block = me - 2 * r
            up(block).wait_recv()

            @pl.when(z < groups - 1)
            def _():
                up(block).start()

            cross(block).start()
            core(block, mine).start()

        @pl.when(z + r < groups)
        def _():
            block = me + 2 * r
            down(block).wait_recv()

            @pl.when(z > 0)
            def _():
                down(block).start()

            cross(block).start()
            core(block, mine).start()

    def each_at(distance, what):
        def one(s, carry):
            g = z + (2 * s - 1) * distance
            inside = jnp.logical_and(g >= 0, g < groups)
            fresh = jnp.logical_or(s == 0, distance > 0)

            @pl.when(jnp.logical_and(distance >= 0, jnp.logical_and(inside, fresh)))
            def _():
                what(g)

            return carry

        lax.fori_loop(0, 2, one, 0)

    def from_across(g):
        block = 2 * g + 1 - x
        cross(block).wait_recv()
        side(block, mine_near).start()
        core(block, mine_near).start()

    def from_beside(g):
        block = 2 * g + 1 - x
        side(block, mine_far).wait_recv()
        core_far(block, mine_far).start()

    def work(g):
        @pl.when(g != z)
        def _():
            core(2 * g + x, other).wait_recv()

        core(2 * g + 1 - x, other_near).wait_recv()
        core_far(2 * g + 1 - x, other_far).wait_recv()
        compute(g)

    def ring(r, carry):
        @pl.when(jnp.logical_and(r > 0, r < groups - 1))
        def _():
            line(r)

        each_at(r - 1, from_across)

        @pl.when(r == 1)
        def _():
            loads[1].wait()
            loads[2].wait()
            lax.fori_loop(0, comps // TILE, prepare, 0)

        each_at(r - 2, work)
        each_at(r - 1, from_beside)

        @pl.when(jnp.logical_and(r > 0, r == groups - 1))
        def _():
            line(r)

        return carry

    lax.fori_loop(0, groups + 2, ring, 0)

    def exchange(turn):
        def to(hop):
            return pltpu.make_async_remote_copy(
                src_ref=stats.at[turn, ce],
                dst_ref=stats.at[turn, ce],
                send_sem=stat_sem.at[turn, 0, hop - 1],
                recv_sem=stat_sem.at[turn, 1, hop - 1],
                device_id={"dp": me, "comp": lax.rem(ce + hop, comp)},
                device_id_type=pl.DeviceIdType.MESH,
            )

        for hop in range(1, comp):
            to(hop).start()
        for hop in range(1, comp):
            to(hop).wait()
        peak = stats[turn, 0, :, 0:1, :]
        for c in range(1, comp):
            peak = jnp.maximum(peak, stats[turn, c, :, 0:1, :])
        summed = jnp.zeros_like(peak)
        for c in range(comp):
            summed += stats[turn, c, :, 1:2, :] * jnp.exp(stats[turn, c, :, 0:1, :] - peak)
        norm[...] = peak + jnp.log(summed)

    exchange(0)

    outs = [
        pltpu.make_async_copy(right_high, right_high_out, local_sem.at[0]),
        pltpu.make_async_copy(right_low, right_low_out, local_sem.at[1]),
    ]
    for out in outs:
        out.start()

    def leave(t):
        rows = pl.ds(pl.multiple_of(t * TILE, TILE), TILE)
        return pltpu.make_async_copy(
            density.at[:, rows, :], density_out.at[:, rows, :], leave_sem.at[t]
        )

    def again(turn, t, carry):
        rows = pl.ds(pl.multiple_of(t * TILE, TILE), TILE)
        shares = shares_of(density, norm, rows)
        counts = jnp.sum(shares, 1, keepdims=True)
        high, low = split(shares)
        offset = jnp.zeros((TILE, 1), jnp.float32)
        for c in range(width // CHUNK):
            centre, var = m_step(
                high, low, right_high, right_low, pl.ds(c * CHUNK, CHUNK), width, counts
            )
            offset += left_of(centre, var, rows, c * CHUNK, width, left_high, left_low)
        logit = jnp.log((counts + 1.0) / total)
        base[rows, :] = logit - 0.5 * (offset + width * LOG_TWO_PI)

        def group(g, carry):
            e_tile(g, t)
            return carry

        lax.fori_loop(0, groups, group, 0)
        if turn == ITERS - 1:
            leave(t).start()
        return carry

    for turn in range(1, ITERS):
        lax.fori_loop(0, comps // TILE, functools.partial(again, turn), 0)

        def each(g, carry, turn=turn):
            stat(turn, g)
            return carry

        lax.fori_loop(0, groups, each, 0)
        exchange(turn)

    norm_out[...] = norm[...]
    lanes = pl.ds(pl.multiple_of(x * rows_here, LANES), rows_here)
    mine_out[...] = norm[z, :, lanes]

    @pl.when(z < groups - 1)
    def _():
        up(me).wait_send()

    @pl.when(z > 0)
    def _():
        down(me).wait_send()

    cross(me).wait_send()

    def drain(block, carry):
        g = block // 2

        @pl.when(jnp.logical_and(block % 2 == x, g < z))
        def _():
            @pl.when(z < groups - 1)
            def _():
                up(block).wait_send()

            cross(block).wait_send()

        @pl.when(jnp.logical_and(block % 2 == x, g > z))
        def _():
            @pl.when(z > 0)
            def _():
                down(block).wait_send()

            cross(block).wait_send()

        @pl.when(jnp.logical_and(block % 2 == x, g != z))
        def _():
            core(block, mine).wait_send()

        @pl.when(block % 2 != x)
        def _():
            side(block, mine_near).wait_send()
            core(block, mine_near).wait_send()
            core_far(block, mine_far).wait_send()

        return carry

    lax.fori_loop(0, dp, drain, 0)

    def left(t, carry):
        leave(t).wait()
        return carry

    lax.fori_loop(0, comps // TILE, left, 0)
    for out in outs:
        out.wait()


def last_kernel(
    total,
    density,
    norm,
    right_high,
    right_low,
    mine,
    centre_out,
    var_out,
    logit_out,
    mine_out,
):
    width = centre_out.shape[1]
    shares = shares_of(density, norm, slice(None))
    counts = jnp.sum(shares, 1, keepdims=True)
    high, low = split(shares)
    for c in range(width // CHUNK):
        at = pl.ds(c * CHUNK, CHUNK)
        centre, var = m_step(high, low, right_high, right_low, at, width, counts)
        centre_out[:, at] = centre
        var_out[:, at] = var
    logit_out[...] = to_row(jnp.log((counts + 1.0) / total))
    mine_out[...] = mine[...]


def fused(dp, comp, points, centres, variances, mix_logits):
    rows_here, width = points.shape
    comps = centres.shape[0]
    groups, pair, every = dp // 2, 2 * rows_here, dp * rows_here
    f32, bf16 = jnp.float32, jnp.bfloat16
    vmem, anyw = pl.BlockSpec(memory_space=pltpu.VMEM), pl.BlockSpec(memory_space=pl.ANY)
    density, high, low, norm, mine = pl.pallas_call(
        functools.partial(em_kernel, dp, comp),
        out_shape=[
            jax.ShapeDtypeStruct((groups, comps, pair), f32),
            jax.ShapeDtypeStruct((every, 2 * width), bf16),
            jax.ShapeDtypeStruct((every, 2 * width), bf16),
            jax.ShapeDtypeStruct((groups, 1, pair), f32),
            jax.ShapeDtypeStruct((1, rows_here), f32),
        ],
        in_specs=[anyw, anyw, anyw, vmem],
        out_specs=[anyw, anyw, anyw, vmem, vmem],
        scratch_shapes=[
            pltpu.VMEM((groups, pair, width), f32),
            pltpu.VMEM((comps, width), f32),
            pltpu.VMEM((comps, width), f32),
            pltpu.VMEM((comps, 2 * width), bf16),
            pltpu.VMEM((comps, 2 * width), bf16),
            pltpu.VMEM((every, 2 * width), bf16),
            pltpu.VMEM((every, 2 * width), bf16),
            pltpu.VMEM((groups, comps, pair), f32),
            pltpu.VMEM((comps, 1), f32),
            pltpu.VMEM((groups, 1, pair), f32),
            pltpu.VMEM((ITERS, comp, groups, 2, pair), f32),
            pltpu.SemaphoreType.DMA((3,)),
            pltpu.SemaphoreType.DMA((11, dp)),
            pltpu.SemaphoreType.DMA((ITERS, 2, comp - 1)),
            pltpu.SemaphoreType.DMA((comps // TILE,)),
        ],
        compiler_params=pltpu.CompilerParams(
            collective_id=0, has_side_effects=True, vmem_limit_bytes=VMEM_BYTES
        ),
        name="em",
    )(points, centres, variances, mix_logits[None, :])
    total = float(every + comps * comp)
    whole = lambda *shape: pl.BlockSpec(shape, lambda t: (0,) * len(shape))
    centre, var, logit, log_norm = pl.pallas_call(
        functools.partial(last_kernel, total),
        grid=(comps // TILE,),
        out_shape=[
            jax.ShapeDtypeStruct((comps, width), f32),
            jax.ShapeDtypeStruct((comps, width), f32),
            jax.ShapeDtypeStruct((1, comps), f32),
            jax.ShapeDtypeStruct((1, rows_here), f32),
        ],
        in_specs=[
            pl.BlockSpec((groups, TILE, pair), lambda t: (0, t, 0)),
            whole(groups, 1, pair),
            whole(every, 2 * width),
            whole(every, 2 * width),
            whole(1, rows_here),
        ],
        out_specs=[
            pl.BlockSpec((TILE, width), lambda t: (t, 0)),
            pl.BlockSpec((TILE, width), lambda t: (t, 0)),
            pl.BlockSpec((1, TILE), lambda t: (0, t)),
            whole(1, rows_here),
        ],
        compiler_params=pltpu.CompilerParams(vmem_limit_bytes=VMEM_BYTES),
        name="last",
    )(density, norm, high, low, mine)
    return centre, var, logit.reshape(comps), log_norm.reshape(rows_here)


def solution(mesh):
    dp, comp = mesh.shape["dp"], mesh.shape["comp"]

    def body(points, centres, variances, mix_logits):
        rows, width = points.shape
        comps = centres.shape[0]
        every = dp * rows
        need = every * width * 12 + comps * width * 16 + comps * every * 4
        fits = need < VMEM_BYTES * 3 // 4 and dp % 2 == 0 and comp % 4 == 0
        fits = fits and rows % LANES == 0 and width % (4 * LANES) == 0 and comps % TILE == 0
        form = functools.partial(fused, dp, comp) if fits else on_device
        return form(points, centres, variances, mix_logits)

    return jax.shard_map(
        body,
        mesh=mesh,
        in_specs=(P("dp", None), P("comp", None), P("comp", None), P("comp")),
        out_specs=(P("comp", None), P("comp", None), P("comp"), P("dp")),
        check_vma=False,
    )
```
